128 devices in a mesh: leaf: 32 (over x, y, core), chain: 4 (over z).
Axes of the slice: x: 4, y: 4, z: 4, core: 2. Of those that a mesh axis runs over, the one named last changes fastest.
Arguments:
- right_side: float32 [32, 4096, 1024], P('leaf', 'chain'), may hold values from -6 to 6
- lower_rows: bfloat16 [32, 4096, 4096], P('leaf', 'chain'), may hold values from -0.09375 to 0.09375
- block_inverse: bfloat16 [32, 4096, 1024], P('leaf', 'chain'), may hold values from -0.1875 to 0.1875
- ancestor_cols: bfloat16 [32, 3072, 4096], P('leaf', None, 'chain'), may hold values from -0.09375 to 0.09375
- pattern: int32 [32, 24], P('leaf'), may hold values 0 or 1
- ancestor_side: float32 [3072, 1024], P('chain'), may hold values from -24 to 24
- ancestor_inverse: bfloat16 [3072, 768], P('chain'), may hold values from -0.21875 to 0.21875
Outputs:
- solution: float32 [32, 4096, 1024], P('leaf', 'chain')
- ancestor_solution: float32 [4, 768, 1024], P('chain', 'leaf')
The draws below stay inside these ranges and needn't reach their ends.
All inputs are finite; a program needn't handle non-finite values. No bound on the sum of `pattern` on one device may be relied on, other than what follows from the above.
Results may differ from the reference program's by a relative error of at most 0.0065.
Values may be sent and summed in bfloat16 or wider, within the bound.
A program may use at most 128 MiB of HBM per device.

```python
import jax
import jax.numpy as jnp
from jax import lax

F = 4096
A = 3072
R = 1024
ROWBLK = 128
GROUPS = 32
FB = 1024
AB = 768
N_CHAIN = 4


def with_ends(array, rng, low, high):
    longest = array.shape.index(max(array.shape))
    spots = []
    for shift in (0, 1):
        where = [jax.random.randint(jax.random.fold_in(rng, axis), (), 0, length) for axis, length in enumerate(array.shape)]
        where[longest] = (where[longest] + shift) % array.shape[longest]
        spots.append(tuple(where))
    return array.at[spots[0]].set(low).at[spots[1]].set(high)


def level_of(rng, shape, cuts, low, top_value):
    def one(position, parts):
        draws = jax.random.uniform(jax.random.fold_in(jax.random.fold_in(rng, 6), position), (parts,), jnp.float32, low / len(cuts), top_value / len(cuts))
        return jnp.repeat(jnp.exp(draws), shape[position] // parts).reshape((-1,) + (1,) * (len(shape) - position - 1))

    level = one(*cuts[0])
    for cut in cuts[1:]:
        level = level * one(*cut)
    return level


def bell_draw(stream_key, dims, spread, reach, cuts=(), kind=jnp.bfloat16):
    drawn = jax.random.normal(stream_key, dims, jnp.float32) * spread
    if len(cuts) > 0:
        drawn = level_of(stream_key, dims, cuts, -0.22, 0.18) * drawn
    return jnp.clip(drawn, min=-reach, max=reach).astype(kind)


def setup_inputs(seed: int = 0) -> dict:
    seeds = jax.random.split(jax.random.key(seed), 8)
    return {
        "right_side": bell_draw(seeds[0], (GROUPS, F, R), 1.0, 6.0, ((0, 32), (1, 4)), jnp.float32),
        "lower_rows": bell_draw(seeds[1], (GROUPS, F, F), F ** -0.5, 0.09375, ((0, 32), (1, 4))),
        "block_inverse": bell_draw(seeds[2], (GROUPS, F, FB), FB ** -0.5, 0.1875, ((0, 32), (1, 4))),
        "ancestor_cols": bell_draw(seeds[3], (GROUPS, A, F), F ** -0.5, 0.09375, ((0, 32), (2, 4))),
        "pattern": with_ends((jax.random.randint(seeds[4], (GROUPS, A // ROWBLK), 0, 4) < 3).astype(jnp.int32), jax.random.fold_in(seeds[4], 1), 0, 1),
        "ancestor_side": bell_draw(seeds[5], (A, R), 4.0, 24.0, ((0, 4),), jnp.float32),
        "ancestor_inverse": bell_draw(seeds[6], (A, AB), AB ** -0.5, 0.21875, ((0, 4),)),
    }


def wide_dot(left, right):
    return jnp.dot(left.astype(jnp.float32), right.astype(jnp.float32), precision=lax.Precision.HIGHEST)


def one_front(carry, inputs):
    lower, inverse, columns, rhs_rows, flags = inputs
    block_rows = F // N_CHAIN
    solved_list = []
    rounded_list = []
    for chain_step in range(N_CHAIN):
        low = chain_step * block_rows
        high = low + block_rows
        pending = jnp.zeros((block_rows, R), jnp.float32)
        for earlier in range(chain_step):
            pending = pending + wide_dot(lower[low:high, earlier * block_rows:(earlier + 1) * block_rows], rounded_list[earlier])
        solved = wide_dot(inverse[low:high], (rhs_rows[low:high] - pending).astype(jnp.bfloat16))
        solved_list.append(solved)
        rounded_list.append(solved.astype(jnp.bfloat16))
    rounded = jnp.concatenate(rounded_list, axis=0)
    row_flags = jnp.repeat(flags.astype(jnp.float32), ROWBLK)
    update = wide_dot(columns, rounded) * row_flags[:, None]
    return carry + update, jnp.concatenate(solved_list, axis=0)


def reference(right_side, lower_rows, block_inverse, ancestor_cols, pattern, ancestor_side, ancestor_inverse):
    start_sum = jnp.zeros((A, R), jnp.float32)
    summed, solution = lax.scan(one_front, start_sum, (lower_rows, block_inverse, ancestor_cols, right_side, pattern))
    block_rows = A // N_CHAIN
    results = []
    for chain_step in range(N_CHAIN):
        low = chain_step * block_rows
        high = low + block_rows
        results.append(wide_dot(ancestor_inverse[low:high], (ancestor_side[low:high] - summed[low:high]).astype(jnp.bfloat16)))
    return solution, jnp.stack(results, axis=0)
```

```python
import jax
import jax.numpy as jnp
from jax import lax
from jax.experimental import pallas as pl
from jax.experimental.pallas import tpu as pltpu
from jax.sharding import PartitionSpec as P

MESH = pl.DeviceIdType.MESH
ROWBLK = 128
NK = 8
W = 128
NA = 3
AHEAD = 4
B16 = jnp.bfloat16
F32 = jnp.float32


def dot(a, b):
    return jnp.dot(a, b, preferred_element_type=F32)


def wait(ref, sem):
    pltpu.make_async_copy(ref, ref, sem).wait()


def send(src, dst, ssem, rsem, leaf, chain):
    pltpu.make_async_remote_copy(
        src_ref=src,
        dst_ref=dst,
        send_sem=ssem,
        recv_sem=rsem,
        device_id=(leaf, chain),
        device_id_type=MESH,
    ).start()


def kernel(
    flags, rhs_hbm, low_hbm, inv_hbm, cols_hbm, side_hbm, ainv_hbm,
    sol_hbm, anc_hbm,
    rv, lv, iv, cv, av, sv, acc, blk, own, sx, rx, s1, r1, s2, r2, s3, r3, st, tt, ov,
    rhs_sem, in_sem, out_sem, anc_sem,
    blk_send, blk_recv, x_send, x_recv, s1_send, s1_recv, s2_send, s2_recv,
    z_send, z_recv, ag_same, ag_other, ag_recv,
):
    me = lax.axis_index("leaf")
    z = lax.axis_index("chain")
    core = lax.rem(me, 2)
    chip = lax.div(me, 2)
    x = lax.div(chip, 4)
    y = lax.rem(chip, 4)
    f = x + core * (y - x)
    g = y + core * (x - y)

    def chip_of(ff, gg):
        a, b = ff * 4 + gg, gg * 4 + ff
        return a + core * (b - a)

    chip_rows = pl.ds(pl.multiple_of(chip * 48, 48), 48)

    def rhs_load(k):
        return pltpu.make_async_copy(
            rhs_hbm.at[0, :, pl.ds(k * W, W)], rv.at[k], rhs_sem.at[k]
        )

    def low_load(j):
        return pltpu.make_async_copy(
            low_hbm.at[0, :, pl.ds(j * 1024, 1024)], lv.at[j], in_sem.at[j]
        )

    inv_load = pltpu.make_async_copy(inv_hbm.at[0], iv, in_sem.at[3])
    cols_load = pltpu.make_async_copy(cols_hbm.at[0], cv, in_sem.at[4])
    side_load = pltpu.make_async_copy(side_hbm.at[chip_rows, :], sv, in_sem.at[5])
    ainv_load = pltpu.make_async_copy(ainv_hbm.at[chip_rows, :], av, in_sem.at[6])
    inv_load.start()
    for k in range(NK):
        rhs_load(k).start()
    for j in range(3):
        @pl.when(z > j)
        def _():
            low_load(j).start()
    cols_load.start()
    side_load.start()
    ainv_load.start()

    barrier = pltpu.get_barrier_semaphore()

    @pl.loop(1, 32)
    def _(i):
        pl.semaphore_signal(
            barrier, inc=1, device_id=(lax.rem(me + i, 32), z), device_id_type=MESH
        )

    @pl.loop(1, 4)
    def _(i):
        pl.semaphore_signal(
            barrier, inc=1, device_id=(me, lax.rem(z + i, 4)), device_id_type=MESH
        )

    pl.semaphore_wait(barrier, 34)

    def send_block(j, k, slot, to):
        send(blk.at[j, k], blk.at[j, k], blk_send.at[slot, k], blk_recv.at[j, k], me, to)

    def pass_block0(k):
        wait(blk.at[0, k], blk_recv.at[0, k])
        send_block(0, k, 2, 2)

    inv_load.wait()
    for j in range(3):
        @pl.when(z > j)
        def _():
            low_load(j).wait()

    @pl.when(z == 3)
    def _():
        @pl.loop(0, AHEAD)
        def _(k):
            pass_block0(k)

    def chain(k):
        wait(rv.at[k], rhs_sem.at[k])
        acc[...] = rv[k]

        @pl.loop(0, z)
        def _(j):
            @pl.when(jnp.logical_or(z != 3, j != 0))
            def _():
                wait(blk.at[j, k], blk_recv.at[j, k])

            @pl.when(jnp.logical_and(jnp.logical_and(z == 2, j == 1), k < NA))
            def _():
                send_block(1, k, 2, 3)

            acc[...] -= dot(lv[j], blk[j, k])

        solved = dot(iv[...], acc[...].astype(B16))
        blk[z, k] = solved.astype(B16)
        rv[k] = solved

        @pl.when(z < 3)
        def _():
            send_block(z, k, 0, z + 1)

        @pl.when(jnp.logical_or(z == 0, jnp.logical_and(z == 1, k >= NA)))
        def _():
            send_block(z, k, 1, lax.rem(z + 3, 4))

        pltpu.make_async_copy(
            rv.at[k],
            sol_hbm.at[0, :, pl.ds(pl.multiple_of(k * W, W), W)],
            out_sem.at[k],
        ).start()

    def mask_columns():
        cols_load.wait()

        @pl.loop(0, 24)
        def _(i):
            rows = pl.ds(pl.multiple_of(i * ROWBLK, ROWBLK), ROWBLK)
            cv[rows, :] = cv[rows, :] * flags[0, i].astype(F32).astype(B16)

    def product(k):
        solved = blk[z, k]
        for i in range(2):
            rows = pl.ds(pl.multiple_of((1 - core) * 1536 + i * 768, 768), 768)
            sx[k, i * 768:(i + 1) * 768, :] = dot(cv[rows, :], solved).astype(B16)
        send(sx.at[k], rx.at[k], x_send.at[k], x_recv.at[k], me + 1 - 2 * core, z)
        for i in range(2):
            rows = pl.ds(pl.multiple_of(core * 1536 + i * 768, 768), 768)
            own[i * 768:(i + 1) * 768, :] = dot(cv[rows, :], solved)

    def pair_sum(k):
        wait(rx.at[k], x_recv.at[k])
        for ci in range(2):
            for ff in range(4):
                for gg in range(4):
                    rows = pl.ds(pl.multiple_of(ci * 768 + chip_of(ff, gg) * 48, 48), 48)
                    total = own[rows, :] + rx[k, rows, :].astype(F32)
                    at = ci * 192 + gg * 48
                    s1[k, ff, at:at + 48, :] = total.astype(B16)
        for d in range(1, 4):
            to = lax.rem(f + d, 4)
            send(
                s1.at[k, to], r1.at[k, d - 1], s1_send.at[k], s1_recv.at[k],
                chip_of(to, g) * 2 + core, z,
            )

    def first_sum(k):
        wait(r1.at[k], s1_recv.at[k])
        for ci in range(2):
            for gg in range(4):
                at = ci * 192 + gg * 48
                total = s1[k, f, at:at + 48, :].astype(F32)
                for d in range(3):
                    total += r1[k, d, at:at + 48, :].astype(F32)
                s2[k, gg, ci * 48:(ci + 1) * 48, :] = total.astype(B16)
        for d in range(1, 4):
            to = lax.rem(g + d, 4)
            send(
                s2.at[k, to], r2.at[k, d - 1], s2_send.at[k], s2_recv.at[k],
                chip_of(f, to) * 2 + core, z,
            )

    def second_sum(k):
        wait(r2.at[k], s2_recv.at[k])
        for ci in range(2):
            at = ci * 48
            total = s2[k, g, at:at + 48, :].astype(F32)
            for d in range(3):
                total += r2[k, d, at:at + 48, :].astype(F32)
            s3[k, ci] = total
            owner = core * 2 + ci
            away = lax.rem(owner - z + 4, 4)

            @pl.when(away != 0)
            def _():
                send(
                    s3.at[k, ci], r3.at[k, away - 1], z_send.at[k, ci], z_recv.at[k],
                    me, owner,
                )

    mine = lax.div(z, 2) == core

    def last_sum(k):
        wait(r3.at[k], z_recv.at[k])
        total = s3[k, z - 2 * core]
        for d in range(3):
            total += r3[k, d]
        here = sv[:, pl.ds(pl.multiple_of(k * W, W), W)]
        st[k] = (here - total).astype(B16)

    def share(batch, low, high):
        src = st.at[low:high]
        dst = tt.at[low:high, chip_rows, :]

        @pl.loop(0, 16)
        def _(i):
            to = lax.rem(me + 2 * i + 1, 32)
            send(src, dst, ag_other.at[batch], ag_recv.at[batch], to, z)

        @pl.loop(1, 16)
        def _(i):
            to = lax.rem(me + 2 * i, 32)
            send(src, dst, ag_same.at[batch], ag_recv.at[batch], to, z)

        pltpu.make_async_copy(src, dst, ag_recv.at[batch]).start()

    @pl.loop(0, NK)
    def _(k):
        @pl.when(jnp.logical_and(z == 3, k + AHEAD < NK))
        def _():
            pass_block0(k + AHEAD)

        chain(k)

        @pl.when(k == 0)
        def _():
            mask_columns()

        product(k)

        @pl.when(k >= 1)
        def _():
            first_sum(k - 1)

        pair_sum(k)

        @pl.when(k >= 2)
        def _():
            second_sum(k - 2)

    @pl.when(z == 0)
    def _():
        @pl.loop(NA, NK)
        def _(k):
            wait(blk.at[1, k], blk_recv.at[1, k])
            send_block(1, k, 2, 3)

    side_load.wait()
    ainv_load.wait()
    second_sum(NK - 2)

    def early():
        @pl.loop(0, NK - 1)
        def _(k):
            last_sum(k)

        share(0, 0, NK - 1)

    @pl.when(jnp.logical_and(mine, z == 3))
    def _():
        early()

    first_sum(NK - 1)
    second_sum(NK - 1)

    @pl.when(jnp.logical_and(mine, z != 3))
    def _():
        early()

    @pl.when(mine)
    def _():
        last_sum(NK - 1)
        share(1, NK - 1, NK)

    for batch, low, high in ((0, 0, NK - 1), (1, NK - 1, NK)):
        wait(tt.at[low:high], ag_recv.at[batch])
        for k in range(low, high):
            ov[:, k * W:(k + 1) * W] = dot(av[...], tt[k])
    anc_out = pltpu.make_async_copy(
        ov.at[pl.ds(pl.multiple_of(core * 24, 24), 24), :], anc_hbm.at[0], anc_sem
    )
    anc_out.start()

    @pl.loop(0, NK)
    def _(k):
        wait(rv.at[k], out_sem.at[k])

        @pl.when(z < 3)
        def _():
            wait(blk.at[0, k], blk_send.at[0, k])

        @pl.when(jnp.logical_or(z == 0, jnp.logical_and(z == 1, k >= NA)))
        def _():
            wait(blk.at[0, k], blk_send.at[1, k])

        @pl.when(jnp.logical_or(
            z == 3,
            jnp.logical_or(jnp.logical_and(z == 2, k < NA), jnp.logical_and(z == 0, k >= NA)),
        ))
        def _():
            wait(blk.at[0, k], blk_send.at[2, k])

        wait(sx.at[k], x_send.at[k])
        wait(r1.at[k], s1_send.at[k])
        wait(r2.at[k], s2_send.at[k])
        for ci in range(2):
            @pl.when(core * 2 + ci != z)
            def _():
                wait(s3.at[k, ci], z_send.at[k, ci])

    @pl.when(mine)
    def _():
        for batch, low, high in ((0, 0, NK - 1), (1, NK - 1, NK)):
            wait(tt.at[low:high], ag_other.at[batch])
            wait(tt.at[low:high, 0:720, :], ag_same.at[batch])

    anc_out.wait()


def local(
    right_side, lower_rows, block_inverse, ancestor_cols, pattern, ancestor_side, ancestor_inverse
):
    any_spec = pl.BlockSpec(memory_space=pl.ANY)
    vmem, dma = pltpu.VMEM, pltpu.SemaphoreType.DMA
    return pl.pallas_call(
        kernel,
        out_shape=(
            jax.ShapeDtypeStruct((1, 1024, 1024), F32),
            jax.ShapeDtypeStruct((1, 24, 1024), F32),
        ),
        in_specs=[pl.BlockSpec(memory_space=pltpu.SMEM)] + [any_spec] * 6,
        out_specs=(any_spec, any_spec),
        scratch_shapes=[
            vmem((NK, 1024, W), F32),
            vmem((3, 1024, 1024), B16),
            vmem((1024, 1024), B16),
            vmem((3072, 1024), B16),
            vmem((48, 768), B16),
            vmem((48, 1024), F32),
            vmem((1024, W), F32),
            vmem((4, NK, 1024, W), B16),
            vmem((1536, W), F32),
            vmem((NK, 1536, W), B16),
            vmem((NK, 1536, W), B16),
            vmem((NK, 4, 384, W), B16),
            vmem((NK, 3, 384, W), B16),
            vmem((NK, 4, 96, W), B16),
            vmem((NK, 3, 96, W), B16),
            vmem((NK, 2, 48, W), F32),
            vmem((NK, 3, 48, W), F32),
            vmem((NK, 48, W), B16),
            vmem((NK, 768, W), B16),
            vmem((48, 1024), F32),
            dma((NK,)),
            dma((7,)),
            dma((NK,)),
            dma,
            dma((3, NK)),
            dma((4, NK)),
            dma((NK,)), dma((NK,)),
            dma((NK,)), dma((NK,)),
            dma((NK,)), dma((NK,)),
            dma((NK, 2)), dma((NK,)),
            dma((2,)), dma((2,)), dma((2,)),
        ],
        compiler_params=pltpu.CompilerParams(
            collective_id=0, has_side_effects=True, vmem_limit_bytes=60 * 1024 * 1024
        ),
        name="solve",
    )(pattern, right_side, lower_rows, block_inverse, ancestor_cols, ancestor_side, ancestor_inverse)


def solution(mesh):
    return jax.shard_map(
        local,
        mesh=mesh,
        in_specs=(
            P("leaf", "chain", None),
            P("leaf", "chain", None),
            P("leaf", "chain", None),
            P("leaf", None, "chain"),
            P("leaf", None),
            P("chain", None),
            P("chain", None),
        ),
        out_specs=(P("leaf", "chain", None), P("chain", "leaf", None)),
        check_vma=False,
    )
```

```python
import jax
import jax.numpy as jnp
from jax import lax
from jax.experimental import pallas as pl
from jax.experimental.pallas import tpu as pltpu
from jax.sharding import PartitionSpec as P

MESH = pl.DeviceIdType.MESH
ROWBLK = 128
NK = 8
W = 128
NA = 3
AHEAD = 5
B16 = jnp.bfloat16
F32 = jnp.float32


def dot(a, b):
    return jnp.dot(a, b, preferred_element_type=F32)


def wait(ref, sem):
    pltpu.make_async_copy(ref, ref, sem).wait()


def send(src, dst, ssem, rsem, leaf, chain):
    pltpu.make_async_remote_copy(
        src_ref=src,
        dst_ref=dst,
        send_sem=ssem,
        recv_sem=rsem,
        device_id=(leaf, chain),
        device_id_type=MESH,
    ).start()


def kernel(
    flags, rhs_hbm, low_hbm, inv_hbm, cols_hbm, side_hbm, ainv_hbm,
    sol, anc,
    lv, iv, cv, av, sv, blk, own, sx, rx, s1, r1, s2, r2, s3, r3, st, tf, ov,
    rhs_sem, in_sem,
    blk_send, blk_recv, x_send, x_recv, s1_send, s1_recv, s2_send, s2_recv,
    z_send, z_recv, ag_send, ag_recv, o_send, o_recv,
):
    me = lax.axis_index("leaf")
    z = lax.axis_index("chain")
    core = lax.rem(me, 2)
    chip = lax.div(me, 2)
    x = lax.div(chip, 4)
    y = lax.rem(chip, 4)
    f = x + core * (y - x)
    g = y + core * (x - y)

    def chip_of(ff, gg):
        a, b = ff * 4 + gg, gg * 4 + ff
        return a + core * (b - a)

    chip_rows = pl.ds(pl.multiple_of(chip * 48, 48), 48)

    def columns_of(k):
        return pl.ds(k * W if isinstance(k, int) else pl.multiple_of(k * W, W), W)

    def rhs_load(k):
        return pltpu.make_async_copy(
            rhs_hbm.at[0, :, columns_of(k)], sol.at[0, :, columns_of(k)], rhs_sem.at[k]
        )

    def low_load(j):
        return pltpu.make_async_copy(
            low_hbm.at[0, :, pl.ds(j * 1024, 1024)], lv.at[j], in_sem.at[j]
        )

    inv_load = pltpu.make_async_copy(inv_hbm.at[0], iv, in_sem.at[3])
    def cols_load(half):
        here = pl.ds(pl.multiple_of((half + (1 - 2 * half) * (1 - core)) * 1536, 1536), 1536)
        return pltpu.make_async_copy(
            cols_hbm.at[0, here, :], cv.at[half * 1536:(half + 1) * 1536], in_sem.at[4 + half]
        )

    side_load = pltpu.make_async_copy(side_hbm.at[chip_rows, :], sv, in_sem.at[6])
    ainv_load = pltpu.make_async_copy(ainv_hbm.at[chip_rows, :], av, in_sem.at[7])
    inv_load.start()
    rhs_load(0).start()

    barrier = pltpu.get_barrier_semaphore()

    def greet(leaf, chain):
        pl.semaphore_signal(barrier, inc=1, device_id=(leaf, chain), device_id_type=MESH)

    partner = me + 1 - 2 * core
    greet(partner, z)
    for d in range(1, 4):
        greet(me, lax.rem(z + d, 4))

    @pl.loop(1, 16)
    def _(i):
        greet(lax.rem(me + 2 * i, 32), z)

    def solve(k):
        solved = dot(iv[...], sol[0, :, columns_of(k)].astype(B16))
        blk[z, k] = solved.astype(B16)
        sol[0, :, columns_of(k)] = solved

    def send_block(j, k, slot, to):
        send(blk.at[j, k], blk.at[j, k], blk_send.at[slot, k], blk_recv.at[j, k], me, to)

    def send_solved(k):
        @pl.when(z < 3)
        def _():
            send_block(z, k, 0, z + 1)

        @pl.when(jnp.logical_or(z == 0, jnp.logical_and(z == 1, k >= NA)))
        def _():
            send_block(z, k, 1, lax.rem(z + 3, 4))

    def pass_block0(k):
        wait(blk.at[0, k], blk_recv.at[0, k])
        send_block(0, k, 2, 2)
        sol[0, :, columns_of(k)] -= dot(lv[0], blk[0, k])

    inv_load.wait()
    rhs_load(0).wait()
    for k in range(1, NK):
        rhs_load(k).start()
    for j in range(3):
        @pl.when(z > j)
        def _():
            low_load(j).start()
    cols_load(0).start()
    cols_load(1).start()
    side_load.start()
    ainv_load.start()

    @pl.when(z == 0)
    def _():
        solve(0)

    pl.semaphore_wait(barrier, 19)

    @pl.when(z == 0)
    def _():
        send_solved(0)

    for k in range(1, NK):
        rhs_load(k).wait()

    for j in range(3):
        @pl.when(z > j)
        def _():
            low_load(j).wait()

    @pl.when(z == 3)
    def _():
        @pl.loop(0, AHEAD)
        def _(k):
            pass_block0(k)

    def chain(k):
        @pl.loop(lax.div(z, 3), z)
        def _(j):
            wait(blk.at[j, k], blk_recv.at[j, k])

            @pl.when(jnp.logical_and(jnp.logical_and(z == 2, j == 1), k < NA))
            def _():
                send_block(1, k, 2, 3)

            sol[0, :, columns_of(k)] -= dot(lv[j], blk[j, k])

        @pl.when(z + k > 0)
        def _():
            solve(k)
            send_solved(k)

    def mask_columns():
        for half in range(2):
            cols_load(half).wait()

        @pl.loop(0, 24)
        def _(i):
            rows = pl.ds(pl.multiple_of(i * ROWBLK, ROWBLK), ROWBLK)
            entry = lax.rem(i + 12 * (1 - core), 24)
            cv[rows, :] = cv[rows, :] * flags[0, entry].astype(F32).astype(B16)

    def product(chunks):
        solved = jnp.concatenate([blk[z, k] for k in chunks], axis=1)
        part = dot(cv[0:1536, :], solved)
        for i, k in enumerate(chunks):
            sx[k] = part[:, i * W:(i + 1) * W].astype(B16)
            send(sx.at[k], rx.at[k], x_send.at[k], x_recv.at[k], partner, z)
        part = dot(cv[1536:3072, :], solved)
        for i in range(len(chunks)):
            own[i] = part[:, i * W:(i + 1) * W]

    def pair_sum(k, slot):
        wait(rx.at[k], x_recv.at[k])
        for ff in range(4):
            for ci in range(2):
                for gg in range(4):
                    rows = pl.ds(pl.multiple_of(ci * 768 + chip_of(ff, gg) * 48, 48), 48)
                    total = own[slot, rows, :] + rx[k, rows, :].astype(F32)
                    at = ci * 192 + gg * 48
                    s1[k, ff, at:at + 48, :] = total.astype(B16)
        for d in range(1, 4):
            to = lax.rem(f + d, 4)
            send(
                s1.at[k, to], r1.at[k, d - 1], s1_send.at[k], s1_recv.at[k],
                chip_of(to, g) * 2 + core, z,
            )

    def first_sum(k):
        wait(r1.at[k], s1_recv.at[k])
        for ci in range(2):
            for gg in range(4):
                at = ci * 192 + gg * 48
                total = s1[k, f, at:at + 48, :].astype(F32)
                for d in range(3):
                    total += r1[k, d, at:at + 48, :].astype(F32)
                s2[k, gg, ci * 48:(ci + 1) * 48, :] = total.astype(B16)
        for d in range(1, 4):
            to = lax.rem(g + d, 4)
            send(
                s2.at[k, to], r2.at[k, d - 1], s2_send.at[k], s2_recv.at[k],
                chip_of(f, to) * 2 + core, z,
            )

    def second_sum(k):
        wait(r2.at[k], s2_recv.at[k])
        for ci in range(2):
            at = ci * 48
            total = s2[k, g, at:at + 48, :].astype(F32)
            for d in range(3):
                total += r2[k, d, at:at + 48, :].astype(F32)
            s3[k, ci] = total
            owner = core * 2 + ci
            away = lax.rem(owner - z + 4, 4)

            @pl.when(away != 0)
            def _():
                send(
                    s3.at[k, ci], r3.at[k, away - 1], z_send.at[k, ci], z_recv.at[k],
                    me, owner,
                )

    mine = lax.div(z, 2) == core

    def last_sum(k):
        wait(r3.at[k], z_recv.at[k])
        total = s3[k, z - 2 * core]
        for d in range(3):
            total += r3[k, d]
        here = sv[:, pl.ds(pl.multiple_of(k * W, W), W)]
        st[k] = (here - total).astype(B16)

        @pl.loop(1, 16)
        def _(i):
            to = lax.rem(me + 2 * i, 32)
            send(st.at[k], tf.at[k, chip], ag_send.at[k], ag_recv.at[k], to, z)

        tf[k, chip] = st[k]

    def finish(k):
        wait(tf.at[k, 0:15], ag_recv.at[k])
        result = dot(av[...], jnp.concatenate([tf[k, i] for i in range(16)], axis=0))
        ov[k, 0] = result[:24]
        ov[k, 1] = result[24:]
        send(
            ov.at[k, 1 - core], anc.at[0, :, columns_of(k)], o_send.at[k], o_recv.at[k],
            partner, z,
        )
        anc[0, :, columns_of(k)] = ov[k, core]

    def last_plane(step, chunks):
        @pl.when(jnp.logical_and(mine, z == 3))
        def _():
            for k in chunks:
                step(k)

    @pl.loop(0, 3)
    def _(m):
        for i in range(2):
            k = m * 2 + i

            chain(k)

            @pl.when(jnp.logical_and(z == 3, k + AHEAD < NK))
            def _():
                pass_block0(k + AHEAD)

        @pl.when(m == 0)
        def _():
            mask_columns()
            side_load.wait()
            ainv_load.wait()

        product((m * 2, m * 2 + 1))

        @pl.when(m >= 1)
        def _():
            for i in range(2):
                first_sum(m * 2 - 2 + i)

        for i in range(2):
            pair_sum(m * 2 + i, i)

        @pl.when(m >= 2)
        def _():
            for i in range(2):
                second_sum(m * 2 - 4 + i)

            last_plane(last_sum, (0, 1))

    chain(6)
    product((6,))
    second_sum(2)
    second_sum(3)
    pair_sum(6, 0)
    last_plane(last_sum, (2, 3))
    chain(7)
    product((7,))
    first_sum(4)
    first_sum(5)
    pair_sum(7, 0)

    @pl.when(z == 0)
    def _():
        @pl.loop(NA, NK)
        def _(k):
            wait(blk.at[1, k], blk_recv.at[1, k])
            send_block(1, k, 2, 3)

    first_sum(6)
    second_sum(4)
    second_sum(5)
    first_sum(7)
    last_plane(last_sum, (4, 5))
    second_sum(6)
    last_plane(last_sum, (6,))
    second_sum(7)

    @pl.when(jnp.logical_and(mine, z != 3))
    def _():
        @pl.loop(0, NK - 1)
        def _(k):
            last_sum(k)

            @pl.when(k >= 1)
            def _():
                finish(k - 1)

    @pl.when(mine)
    def _():
        last_sum(7)

    last_plane(finish, range(0, 6))

    @pl.when(mine)
    def _():
        finish(6)
        finish(7)

    @pl.loop(0, NK)
    def _(k):
        @pl.when(z < 3)
        def _():
            wait(blk.at[0, k], blk_send.at[0, k])

        @pl.when(jnp.logical_or(z == 0, jnp.logical_and(z == 1, k >= NA)))
        def _():
            wait(blk.at[0, k], blk_send.at[1, k])

        @pl.when(jnp.logical_or(
            z == 3,
            jnp.logical_or(jnp.logical_and(z == 2, k < NA), jnp.logical_and(z == 0, k >= NA)),
        ))
        def _():
            wait(blk.at[0, k], blk_send.at[2, k])

        wait(sx.at[k], x_send.at[k])
        wait(r1.at[k], s1_send.at[k])
        wait(r2.at[k], s2_send.at[k])
        for ci in range(2):
            @pl.when(core * 2 + ci != z)
            def _():
                wait(s3.at[k, ci], z_send.at[k, ci])

        @pl.when(mine)
        def _():
            wait(tf.at[k, 0:15], ag_send.at[k])
            wait(ov.at[k, 0], o_send.at[k])

        @pl.when(jnp.logical_not(mine))
        def _():
            wait(ov.at[k, 0], o_recv.at[k])


def local(
    right_side, lower_rows, block_inverse, ancestor_cols, pattern, ancestor_side, ancestor_inverse
):
    any_spec = pl.BlockSpec(memory_space=pl.ANY)
    vmem, dma = pltpu.VMEM, pltpu.SemaphoreType.DMA
    return pl.pallas_call(
        kernel,
        out_shape=(
            pltpu.VMEM((1, 1024, 1024), F32),
            pltpu.VMEM((1, 24, 1024), F32),
        ),
        in_specs=[pl.BlockSpec(memory_space=pltpu.SMEM)] + [any_spec] * 6,
        out_specs=(pl.BlockSpec(memory_space=vmem),) * 2,
        scratch_shapes=[
            vmem((3, 1024, 1024), B16),
            vmem((1024, 1024), B16),
            vmem((3072, 1024), B16),
            vmem((48, 768), B16),
            vmem((48, 1024), F32),
            vmem((4, NK, 1024, W), B16),
            vmem((2, 1536, W), F32),
            vmem((NK, 1536, W), B16),
            vmem((NK, 1536, W), B16),
            vmem((NK, 4, 384, W), B16),
            vmem((NK, 3, 384, W), B16),
            vmem((NK, 4, 96, W), B16),
            vmem((NK, 3, 96, W), B16),
            vmem((NK, 2, 48, W), F32),
            vmem((NK, 3, 48, W), F32),
            vmem((NK, 48, W), B16),
            vmem((NK, 16, 48, W), B16),
            vmem((NK, 2, 24, W), F32),
            dma((NK,)),
            dma((8,)),
            dma((3, NK)),
            dma((4, NK)),
            dma((NK,)), dma((NK,)),
            dma((NK,)), dma((NK,)),
            dma((NK,)), dma((NK,)),
            dma((NK, 2)), dma((NK,)),
            dma((NK,)), dma((NK,)),
            dma((NK,)), dma((NK,)),
        ],
        compiler_params=pltpu.CompilerParams(
            collective_id=0, has_side_effects=True, vmem_limit_bytes=52 * 1024 * 1024
        ),
        name="solve",
    )(pattern, right_side, lower_rows, block_inverse, ancestor_cols, ancestor_side, ancestor_inverse)


def solution(mesh):
    return jax.shard_map(
        local,
        mesh=mesh,
        in_specs=(
            P("leaf", "chain", None),
            P("leaf", "chain", None),
            P("leaf", "chain", None),
            P("leaf", None, "chain"),
            P("leaf", None),
            P("chain", None),
            P("chain", None),
        ),
        out_specs=(P("leaf", "chain", None), P("chain", "leaf", None)),
        check_vma=False,
    )
```

```python
import jax
import jax.numpy as jnp
from jax import lax
from jax.experimental import pallas as pl
from jax.experimental.pallas import tpu as pltpu
from jax.sharding import PartitionSpec as P

MESH = pl.DeviceIdType.MESH
ROWBLK = 128
NK = 8
W = 128
NA = 3
AHEAD = 5
B16 = jnp.bfloat16
F32 = jnp.float32


def dot(a, b):
    return jnp.dot(a, b, preferred_element_type=F32)


def wait(ref, sem):
    pltpu.make_async_copy(ref, ref, sem).wait()


def send(src, dst, ssem, rsem, leaf, chain):
    pltpu.make_async_remote_copy(
        src_ref=src,
        dst_ref=dst,
        send_sem=ssem,
        recv_sem=rsem,
        device_id=(leaf, chain),
        device_id_type=MESH,
    ).start()


def kernel(
    flags, rhs_hbm, low_hbm, inv_hbm, cols_hbm, side_hbm, ainv_hbm,
    sol, anc,
    lv, iv, cv, av, sv, blk, own, sx, rx, s1, r1, s2, r2, s3, r3, rw, st, tf, ov,
    rhs_sem, in_sem,
    blk_send, blk_recv, x_send, x_recv, s1_send, s1_recv, s2_send, s2_recv,
    z_send, z_recv, w_send, w_recv, ag_send, ag_recv, o_send, o_recv,
):
    me = lax.axis_index("leaf")
    z = lax.axis_index("chain")
    core = lax.rem(me, 2)
    chip = lax.div(me, 2)
    x = lax.div(chip, 4)
    y = lax.rem(chip, 4)
    f = x + core * (y - x)
    g = y + core * (x - y)

    def chip_of(ff, gg):
        a, b = ff * 4 + gg, gg * 4 + ff
        return a + core * (b - a)

    chip_rows = pl.ds(pl.multiple_of(chip * 48, 48), 48)

    def columns_of(k):
        return pl.ds(k * W if isinstance(k, int) else pl.multiple_of(k * W, W), W)

    def rhs_load(k):
        return pltpu.make_async_copy(
            rhs_hbm.at[0, :, columns_of(k)], sol.at[0, :, columns_of(k)], rhs_sem.at[k]
        )

    def low_load(j):
        return pltpu.make_async_copy(
            low_hbm.at[0, :, pl.ds(j * 1024, 1024)], lv.at[j], in_sem.at[j]
        )

    inv_load = pltpu.make_async_copy(inv_hbm.at[0], iv, in_sem.at[3])
    def cols_load(half):
        here = pl.ds(pl.multiple_of((half + (1 - 2 * half) * (1 - core)) * 1536, 1536), 1536)
        return pltpu.make_async_copy(
            cols_hbm.at[0, here, :], cv.at[half * 1536:(half + 1) * 1536], in_sem.at[4 + half]
        )

    side_load = pltpu.make_async_copy(side_hbm.at[chip_rows, :], sv, in_sem.at[6])
    ainv_load = pltpu.make_async_copy(ainv_hbm.at[chip_rows, :], av, in_sem.at[7])
    inv_load.start()
    rhs_load(0).start()

    barrier = pltpu.get_barrier_semaphore()

    def greet(leaf, chain):
        pl.semaphore_signal(barrier, inc=1, device_id=(leaf, chain), device_id_type=MESH)

    partner = me + 1 - 2 * core
    greet(partner, z)
    for d in range(1, 4):
        greet(me, lax.rem(z + d, 4))
        greet(chip_of(lax.rem(f + d, 4), g) * 2 + core, z)
        greet(chip_of(f, lax.rem(g + d, 4)) * 2 + core, z)

    def solve(k):
        solved = dot(iv[...], sol[0, :, columns_of(k)].astype(B16))
        blk[z, k] = solved.astype(B16)
        sol[0, :, columns_of(k)] = solved

    def send_block(j, k, slot, to):
        send(blk.at[j, k], blk.at[j, k], blk_send.at[slot, k], blk_recv.at[j, k], me, to)

    def send_solved(k):
        @pl.when(z < 3)
        def _():
            send_block(z, k, 0, z + 1)

        @pl.when(jnp.logical_or(z == 0, jnp.logical_and(z == 1, k >= NA)))
        def _():
            send_block(z, k, 1, lax.rem(z + 3, 4))

    def pass_block0(k):
        wait(blk.at[0, k], blk_recv.at[0, k])
        send_block(0, k, 2, 2)
        sol[0, :, columns_of(k)] -= dot(lv[0], blk[0, k])

    inv_load.wait()
    rhs_load(0).wait()
    for k in range(1, NK):
        rhs_load(k).start()
    for j in range(3):
        @pl.when(z > j)
        def _():
            low_load(j).start()
    cols_load(0).start()
    cols_load(1).start()
    side_load.start()
    ainv_load.start()

    @pl.when(z == 0)
    def _():
        solve(0)

    pl.semaphore_wait(barrier, 10)

    @pl.when(z == 0)
    def _():
        send_solved(0)

    for k in range(1, NK):
        rhs_load(k).wait()

    for j in range(3):
        @pl.when(z > j)
        def _():
            low_load(j).wait()

    @pl.when(z == 3)
    def _():
        @pl.loop(0, AHEAD)
        def _(k):
            pass_block0(k)

    def chain(k):
        @pl.loop(lax.div(z, 3), z)
        def _(j):
            wait(blk.at[j, k], blk_recv.at[j, k])

            @pl.when(jnp.logical_and(jnp.logical_and(z == 2, j == 1), k < NA))
            def _():
                send_block(1, k, 2, 3)

            sol[0, :, columns_of(k)] -= dot(lv[j], blk[j, k])

        @pl.when(z + k > 0)
        def _():
            solve(k)
            send_solved(k)

    def mask_columns():
        for half in range(2):
            cols_load(half).wait()

        @pl.loop(0, 24)
        def _(i):
            rows = pl.ds(pl.multiple_of(i * ROWBLK, ROWBLK), ROWBLK)
            entry = lax.rem(i + 12 * (1 - core), 24)
            cv[rows, :] = cv[rows, :] * flags[0, entry].astype(F32).astype(B16)

    def product(chunks):
        solved = jnp.concatenate([blk[z, k] for k in chunks], axis=1)
        part = dot(cv[0:1536, :], solved)
        for i, k in enumerate(chunks):
            sx[k] = part[:, i * W:(i + 1) * W].astype(B16)
        part = dot(cv[1536:3072, :], solved)
        for i in range(len(chunks)):
            own[i] = part[:, i * W:(i + 1) * W]
        for k in chunks:
            send(sx.at[k], rx.at[k], x_send.at[k], x_recv.at[k], partner, z)

    def pair_sum(k, slot):
        wait(rx.at[k], x_recv.at[k])
        for ff in range(4):
            for ci in range(2):
                for gg in range(4):
                    rows = pl.ds(pl.multiple_of(ci * 768 + chip_of(ff, gg) * 48, 48), 48)
                    total = own[slot, rows, :] + rx[k, rows, :].astype(F32)
                    at = ci * 192 + gg * 48
                    s1[k, ff, at:at + 48, :] = total.astype(B16)
        for d in range(1, 4):
            to = lax.rem(f + d, 4)
            send(
                s1.at[k, to], r1.at[k, d - 1], s1_send.at[k], s1_recv.at[k],
                chip_of(to, g) * 2 + core, z,
            )

    def first_total(k):
        wait(r1.at[k], s1_recv.at[k])
        for ci in range(2):
            for gg in range(4):
                at = ci * 192 + gg * 48
                total = s1[k, f, at:at + 48, :].astype(F32)
                for d in range(3):
                    total += r1[k, d, at:at + 48, :].astype(F32)
                s2[k, gg, ci * 48:(ci + 1) * 48, :] = total.astype(B16)

    def first_sum(k):
        first_total(k)
        for d in range(1, 4):
            to = lax.rem(g + d, 4)
            send(
                s2.at[k, to], r2.at[k, d - 1], s2_send.at[k], s2_recv.at[k],
                chip_of(f, to) * 2 + core, z,
            )

    def wide_send(k):
        first_total(k)
        slot = z * 4 + g
        for ci in range(2):
            owner = core * 2 + ci
            for d in range(4):
                to = lax.rem(g + d, 4)
                piece = s2.at[k, to, ci * 48:(ci + 1) * 48, :]

                def go():
                    send(piece, rw.at[slot], w_send, w_recv, chip_of(f, to) * 2 + core, owner)

                if d > 0:
                    go()
                else:
                    pl.when(owner != z)(go)

                    @pl.when(owner == z)
                    def _():
                        rw[slot] = piece[...]

    def second_sum(k):
        wait(r2.at[k], s2_recv.at[k])
        for ci in range(2):
            at = ci * 48
            total = s2[k, g, at:at + 48, :].astype(F32)
            for d in range(3):
                total += r2[k, d, at:at + 48, :].astype(F32)
            s3[k, ci] = total
            owner = core * 2 + ci
            away = lax.rem(owner - z + 4, 4)

            @pl.when(away != 0)
            def _():
                send(
                    s3.at[k, ci], r3.at[k, away - 1], z_send.at[k, ci], z_recv.at[k],
                    me, owner,
                )

    mine = lax.div(z, 2) == core

    def wide_sum(k):
        wait(rw.at[0:15], w_recv)
        total = rw[0].astype(F32)
        for i in range(1, 16):
            total += rw[i].astype(F32)
        gather(k, total)

    def last_sum(k):
        wait(r3.at[k], z_recv.at[k])
        total = s3[k, z - 2 * core]
        for d in range(3):
            total += r3[k, d]
        gather(k, total)

    def gather(k, total):
        here = sv[:, pl.ds(pl.multiple_of(k * W, W), W)]
        st[k] = (here - total).astype(B16)

        @pl.loop(1, 16)
        def _(i):
            to = lax.rem(me + 2 * i, 32)
            send(st.at[k], tf.at[k, chip], ag_send.at[k], ag_recv.at[k], to, z)

        tf[k, chip] = st[k]

    def finish(k):
        wait(tf.at[k, 0:15], ag_recv.at[k])
        result = dot(av[...], jnp.concatenate([tf[k, i] for i in range(16)], axis=0))
        ov[k, 0] = result[:24]
        ov[k, 1] = result[24:]
        send(
            ov.at[k, 1 - core], anc.at[0, :, columns_of(k)], o_send.at[k], o_recv.at[k],
            partner, z,
        )
        anc[0, :, columns_of(k)] = ov[k, core]

    def last_plane(step, chunks):
        @pl.when(jnp.logical_and(mine, z == 3))
        def _():
            for k in chunks:
                step(k)

    @pl.loop(0, 3)
    def _(m):
        for i in range(2):
            k = m * 2 + i

            chain(k)

            @pl.when(jnp.logical_and(z == 3, k + AHEAD < NK))
            def _():
                pass_block0(k + AHEAD)

        @pl.when(m == 0)
        def _():
            mask_columns()
            side_load.wait()
            ainv_load.wait()

        product((m * 2, m * 2 + 1))

        @pl.when(m >= 1)
        def _():
            for i in range(2):
                first_sum(m * 2 - 2 + i)

        for i in range(2):
            pair_sum(m * 2 + i, i)

        @pl.when(m >= 2)
        def _():
            for i in range(2):
                second_sum(m * 2 - 4 + i)

    chain(6)
    product((6,))
    second_sum(2)
    second_sum(3)
    chain(7)
    pair_sum(6, 0)
    product((7,))
    first_sum(4)
    first_sum(5)
    pair_sum(7, 0)
    second_sum(4)
    second_sum(5)

    @pl.when(z == 0)
    def _():
        @pl.loop(NA, NK)
        def _(k):
            wait(blk.at[1, k], blk_recv.at[1, k])
            send_block(1, k, 2, 3)

    first_sum(6)
    wide_send(7)
    second_sum(6)
    last_plane(last_sum, range(0, 7))

    @pl.when(jnp.logical_and(mine, z != 3))
    def _():
        @pl.loop(0, NK - 1)
        def _(k):
            last_sum(k)

    @pl.when(mine)
    def _():
        wide_sum(7)

        @pl.loop(0, NK)
        def _(k):
            finish(k)

    @pl.when(mine)
    def _():
        wait(rw.at[0:7], w_send)

    @pl.when(jnp.logical_not(mine))
    def _():
        wait(rw.at[0:8], w_send)

    @pl.loop(0, NK)
    def _(k):
        @pl.when(z < 3)
        def _():
            wait(blk.at[0, k], blk_send.at[0, k])

        @pl.when(jnp.logical_or(z == 0, jnp.logical_and(z == 1, k >= NA)))
        def _():
            wait(blk.at[0, k], blk_send.at[1, k])

        @pl.when(jnp.logical_or(
            z == 3,
            jnp.logical_or(jnp.logical_and(z == 2, k < NA), jnp.logical_and(z == 0, k >= NA)),
        ))
        def _():
            wait(blk.at[0, k], blk_send.at[2, k])

        wait(sx.at[k], x_send.at[k])
        wait(r1.at[k], s1_send.at[k])

        @pl.when(k < NK - 1)
        def _():
            wait(r2.at[k], s2_send.at[k])
            for ci in range(2):
                @pl.when(core * 2 + ci != z)
                def _():
                    wait(s3.at[k, ci], z_send.at[k, ci])

        @pl.when(mine)
        def _():
            wait(tf.at[k, 0:15], ag_send.at[k])
            wait(ov.at[k, 0], o_send.at[k])

        @pl.when(jnp.logical_not(mine))
        def _():
            wait(ov.at[k, 0], o_recv.at[k])


def local(
    right_side, lower_rows, block_inverse, ancestor_cols, pattern, ancestor_side, ancestor_inverse
):
    any_spec = pl.BlockSpec(memory_space=pl.ANY)
    vmem, dma = pltpu.VMEM, pltpu.SemaphoreType.DMA
    return pl.pallas_call(
        kernel,
        out_shape=(
            pltpu.VMEM((1, 1024, 1024), F32),
            pltpu.VMEM((1, 24, 1024), F32),
        ),
        in_specs=[pl.BlockSpec(memory_space=pltpu.SMEM)] + [any_spec] * 6,
        out_specs=(pl.BlockSpec(memory_space=vmem),) * 2,
        scratch_shapes=[
            vmem((3, 1024, 1024), B16),
            vmem((1024, 1024), B16),
            vmem((3072, 1024), B16),
            vmem((48, 768), B16),
            vmem((48, 1024), F32),
            vmem((4, NK, 1024, W), B16),
            vmem((2, 1536, W), F32),
            vmem((NK, 1536, W), B16),
            vmem((NK, 1536, W), B16),
            vmem((NK, 4, 384, W), B16),
            vmem((NK, 3, 384, W), B16),
            vmem((NK, 4, 96, W), B16),
            vmem((NK, 3, 96, W), B16),
            vmem((NK, 2, 48, W), F32),
            vmem((NK, 3, 48, W), F32),
            vmem((16, 48, W), B16),
            vmem((NK, 48, W), B16),
            vmem((NK, 16, 48, W), B16),
            vmem((NK, 2, 24, W), F32),
            dma((NK,)),
            dma((8,)),
            dma((3, NK)),
            dma((4, NK)),
            dma((NK,)), dma((NK,)),
            dma((NK,)), dma((NK,)),
            dma((NK,)), dma((NK,)),
            dma((NK, 2)), dma((NK,)),
            dma, dma,
            dma((NK,)), dma((NK,)),
            dma((NK,)), dma((NK,)),
        ],
        compiler_params=pltpu.CompilerParams(
            collective_id=0, has_side_effects=True, vmem_limit_bytes=52 * 1024 * 1024
        ),
        name="solve",
    )(pattern, right_side, lower_rows, block_inverse, ancestor_cols, ancestor_side, ancestor_inverse)


def solution(mesh):
    return jax.shard_map(
        local,
        mesh=mesh,
        in_specs=(
            P("leaf", "chain", None),
            P("leaf", "chain", None),
            P("leaf", "chain", None),
            P("leaf", None, "chain"),
            P("leaf", None),
            P("chain", None),
            P("chain", None),
        ),
        out_specs=(P("leaf", "chain", None), P("chain", "leaf", None)),
        check_vma=False,
    )
```

```python
import jax
import jax.numpy as jnp
from jax import lax
from jax.experimental import pallas as pl
from jax.experimental.pallas import tpu as pltpu
from jax.sharding import PartitionSpec as P

MESH = pl.DeviceIdType.MESH
ROWBLK = 128
NK = 8
W = 128
NA = 3
AHEAD = 5
B16 = jnp.bfloat16
F32 = jnp.float32


def dot(a, b):
    return jnp.dot(a, b, preferred_element_type=F32)


def wait(ref, sem):
    pltpu.make_async_copy(ref, ref, sem).wait()


def send(src, dst, ssem, rsem, leaf, chain):
    pltpu.make_async_remote_copy(
        src_ref=src,
        dst_ref=dst,
        send_sem=ssem,
        recv_sem=rsem,
        device_id=(leaf, chain),
        device_id_type=MESH,
    ).start()


def kernel(
    flags, rhs_hbm, low_hbm, inv_hbm, cols_hbm, side_hbm, ainv_hbm,
    sol, anc,
    lv, iv, cv, av, sv, blk, own, sx, rx, s1, r1, s2, r2, s3, r3, rw, st, tf, ov,
    rhs_sem, in_sem,
    blk_send, blk_recv, x_send, x_recv, s1_send, s1_recv, s2_send, s2_recv,
    z_send, z_recv, w_send, w_recv, ag_send, ag_recv, o_send, o_recv,
):
    me = lax.axis_index("leaf")
    z = lax.axis_index("chain")
    core = lax.rem(me, 2)
    chip = lax.div(me, 2)
    x = lax.div(chip, 4)
    y = lax.rem(chip, 4)
    f = x + core * (y - x)
    g = y + core * (x - y)

    def chip_of(ff, gg):
        a, b = ff * 4 + gg, gg * 4 + ff
        return a + core * (b - a)

    chip_rows = pl.ds(pl.multiple_of(chip * 48, 48), 48)

    def columns_of(k):
        return pl.ds(k * W if isinstance(k, int) else pl.multiple_of(k * W, W), W)

    def rhs_load(k):
        return pltpu.make_async_copy(
            rhs_hbm.at[0, :, columns_of(k)], sol.at[0, :, columns_of(k)], rhs_sem.at[min(k, 1)]
        )

    def low_load(j):
        return pltpu.make_async_copy(
            low_hbm.at[0, :, pl.ds(j * 1024, 1024)], lv.at[j], in_sem.at[j]
        )

    inv_load = pltpu.make_async_copy(inv_hbm.at[0], iv, in_sem.at[3])
    def cols_load(half):
        here = pl.ds(pl.multiple_of((half + (1 - 2 * half) * (1 - core)) * 1536, 1536), 1536)
        return pltpu.make_async_copy(
            cols_hbm.at[0, here, :], cv.at[half * 1536:(half + 1) * 1536], in_sem.at[4 + half]
        )

    side_load = pltpu.make_async_copy(side_hbm.at[chip_rows, :], sv, in_sem.at[6])
    ainv_load = pltpu.make_async_copy(ainv_hbm.at[chip_rows, :], av, in_sem.at[7])
    inv_load.start()
    rhs_load(0).start()

    barrier = pltpu.get_barrier_semaphore()

    def greet(leaf, chain):
        pl.semaphore_signal(barrier, inc=1, device_id=(leaf, chain), device_id_type=MESH)

    partner = me + 1 - 2 * core
    greet(partner, z)
    for d in range(1, 4):
        greet(me, lax.rem(z + d, 4))
        greet(chip_of(lax.rem(f + d, 4), g) * 2 + core, z)
        greet(chip_of(f, lax.rem(g + d, 4)) * 2 + core, z)

    def solve(k):
        solved = dot(iv[...], sol[0, :, columns_of(k)].astype(B16))
        blk[z, k] = solved.astype(B16)
        sol[0, :, columns_of(k)] = solved

    def send_block(j, k, slot, to):
        send(blk.at[j, k], blk.at[j, k], blk_send.at[slot], blk_recv.at[j, k], me, to)

    def send_solved(k):
        @pl.when(z < 3)
        def _():
            send_block(z, k, 0, z + 1)

        @pl.when(jnp.logical_or(z == 0, jnp.logical_and(z == 1, k >= NA)))
        def _():
            send_block(z, k, 1, lax.rem(z + 3, 4))

    def pass_block0(k):
        wait(blk.at[0, k], blk_recv.at[0, k])
        send_block(0, k, 2, 2)
        sol[0, :, columns_of(k)] -= dot(lv[0], blk[0, k])

    inv_load.wait()
    rhs_load(0).wait()
    for k in range(1, NK):
        rhs_load(k).start()
    for j in range(3):
        @pl.when(z > j)
        def _():
            low_load(j).start()
    cols_load(0).start()
    cols_load(1).start()
    side_load.start()
    ainv_load.start()

    @pl.when(z == 0)
    def _():
        solve(0)

    pl.semaphore_wait(barrier, 10)

    @pl.when(z == 0)
    def _():
        send_solved(0)

    wait(sol.at[0, :, W:NK * W], rhs_sem.at[1])

    for j in range(3):
        @pl.when(z > j)
        def _():
            low_load(j).wait()

    @pl.when(z == 3)
    def _():
        @pl.loop(0, AHEAD)
        def _(k):
            pass_block0(k)

    def chain(k):
        @pl.loop(lax.div(z, 3), z)
        def _(j):
            wait(blk.at[j, k], blk_recv.at[j, k])

            @pl.when(jnp.logical_and(jnp.logical_and(z == 2, j == 1), k < NA))
            def _():
                send_block(1, k, 2, 3)

            sol[0, :, columns_of(k)] -= dot(lv[j], blk[j, k])

        @pl.when(z + k > 0)
        def _():
            solve(k)
            send_solved(k)

    def mask_columns():
        for half in range(2):
            cols_load(half).wait()

        @pl.loop(0, 24)
        def _(i):
            rows = pl.ds(pl.multiple_of(i * ROWBLK, ROWBLK), ROWBLK)
            entry = lax.rem(i + 12 * (1 - core), 24)
            cv[rows, :] = cv[rows, :] * flags[0, entry].astype(F32).astype(B16)

    def product(chunks):
        solved = jnp.concatenate([blk[z, k] for k in chunks], axis=1)
        part = dot(cv[0:1536, :], solved)
        for i, k in enumerate(chunks):
            sx[k] = part[:, i * W:(i + 1) * W].astype(B16)
        part = dot(cv[1536:3072, :], solved)
        for i in range(len(chunks)):
            own[i] = part[:, i * W:(i + 1) * W]
        for k in chunks:
            send(sx.at[k], rx.at[k], x_send, x_recv.at[k], partner, z)

    def pair_sum(k, slot):
        wait(rx.at[k], x_recv.at[k])
        for ff in range(4):
            for ci in range(2):
                for gg in range(4):
                    rows = pl.ds(pl.multiple_of(ci * 768 + chip_of(ff, gg) * 48, 48), 48)
                    total = own[slot, rows, :] + rx[k, rows, :].astype(F32)
                    at = ci * 192 + gg * 48
                    s1[k, ff, at:at + 48, :] = total.astype(B16)
        for d in range(1, 4):
            to = lax.rem(f + d, 4)
            send(
                s1.at[k, to], r1.at[k, d - 1], s1_send, s1_recv.at[k],
                chip_of(to, g) * 2 + core, z,
            )

    def first_total(k):
        wait(r1.at[k], s1_recv.at[k])
        for ci in range(2):
            for gg in range(4):
                at = ci * 192 + gg * 48
                total = s1[k, f, at:at + 48, :].astype(F32)
                for d in range(3):
                    total += r1[k, d, at:at + 48, :].astype(F32)
                s2[k, gg, ci * 48:(ci + 1) * 48, :] = total.astype(B16)

    def first_sum(k):
        first_total(k)
        for d in range(1, 4):
            to = lax.rem(g + d, 4)
            send(
                s2.at[k, to], r2.at[k, d - 1], s2_send, s2_recv.at[k],
                chip_of(f, to) * 2 + core, z,
            )

    def wide_send(k):
        first_total(k)
        slot = z * 4 + g
        for ci in range(2):
            owner = core * 2 + ci
            for d in range(4):
                to = lax.rem(g + d, 4)
                piece = s2.at[k, to, ci * 48:(ci + 1) * 48, :]

                def go():
                    send(piece, rw.at[slot], w_send, w_recv, chip_of(f, to) * 2 + core, owner)

                if d > 0:
                    go()
                else:
                    pl.when(owner != z)(go)

                    @pl.when(owner == z)
                    def _():
                        rw[slot] = piece[...]

    def second_sum(k):
        wait(r2.at[k], s2_recv.at[k])
        for ci in range(2):
            at = ci * 48
            total = s2[k, g, at:at + 48, :].astype(F32)
            for d in range(3):
                total += r2[k, d, at:at + 48, :].astype(F32)
            s3[k, ci] = total
            owner = core * 2 + ci
            away = lax.rem(owner - z + 4, 4)

            @pl.when(away != 0)
            def _():
                send(
                    s3.at[k, ci], r3.at[k, away - 1], z_send, z_recv.at[k],
                    me, owner,
                )

    mine = lax.div(z, 2) == core

    def wide_sum(k):
        wait(rw.at[0:15], w_recv)
        total = rw[0].astype(F32)
        for i in range(1, 16):
            total += rw[i].astype(F32)
        gather(k, total)

    def last_sum(k):
        wait(r3.at[k], z_recv.at[k])
        total = s3[k, z - 2 * core]
        for d in range(3):
            total += r3[k, d]
        gather(k, total)

    def gather(k, total):
        here = sv[:, pl.ds(pl.multiple_of(k * W, W), W)]
        st[k] = (here - total).astype(B16)

        @pl.loop(1, 16)
        def _(i):
            to = lax.rem(me + 2 * i, 32)
            send(st.at[k], tf.at[k, chip], ag_send, ag_recv.at[k], to, z)

        tf[k, chip] = st[k]

    def finish(k):
        wait(tf.at[k, 0:15], ag_recv.at[k])
        result = dot(av[...], jnp.concatenate([tf[k, i] for i in range(16)], axis=0))
        ov[k, 0] = result[:24]
        ov[k, 1] = result[24:]
        send(
            ov.at[k, 1 - core], anc.at[0, :, columns_of(k)], o_send, o_recv,
            partner, z,
        )
        anc[0, :, columns_of(k)] = ov[k, core]

    def last_plane(step, chunks):
        @pl.when(jnp.logical_and(mine, z == 3))
        def _():
            for k in chunks:
                step(k)

    @pl.loop(0, 3)
    def _(m):
        for i in range(2):
            k = m * 2 + i

            chain(k)

            @pl.when(jnp.logical_and(z == 3, k + AHEAD < NK))
            def _():
                pass_block0(k + AHEAD)

        @pl.when(m == 0)
        def _():
            mask_columns()
            side_load.wait()
            ainv_load.wait()

        product((m * 2, m * 2 + 1))

        @pl.when(m >= 1)
        def _():
            for i in range(2):
                first_sum(m * 2 - 2 + i)

        for i in range(2):
            pair_sum(m * 2 + i, i)

        @pl.when(m >= 2)
        def _():
            for i in range(2):
                second_sum(m * 2 - 4 + i)
            last_plane(last_sum, (0,))

    chain(6)
    product((6,))
    second_sum(2)
    second_sum(3)
    chain(7)
    pair_sum(6, 0)
    product((7,))
    first_sum(4)
    first_sum(5)
    pair_sum(7, 0)

    @pl.when(z == 0)
    def _():
        @pl.loop(NA, NK)
        def _(k):
            wait(blk.at[1, k], blk_recv.at[1, k])
            send_block(1, k, 2, 3)

    first_sum(6)
    second_sum(4)
    second_sum(5)
    wide_send(7)
    second_sum(6)

    @pl.when(jnp.logical_and(mine, z != 3))
    def _():
        @pl.loop(0, NK - 1)
        def _(k):
            last_sum(k)

    @pl.when(mine)
    def _():
        wide_sum(7)

    last_plane(last_sum, range(1, 7))

    @pl.when(z < 3)
    def _():
        wait(blk.at[0], blk_send.at[0])

    @pl.when(z == 0)
    def _():
        wait(blk.at[0], blk_send.at[1])
        wait(blk.at[0, NA:NK], blk_send.at[2])

    @pl.when(z == 1)
    def _():
        wait(blk.at[0, NA:NK], blk_send.at[1])

    @pl.when(z == 2)
    def _():
        wait(blk.at[0, 0:NA], blk_send.at[2])

    @pl.when(z == 3)
    def _():
        wait(blk.at[0], blk_send.at[2])

    wait(sx, x_send)
    wait(r1, s1_send)
    wait(r2.at[0:NK - 1], s2_send)

    @pl.when(mine)
    def _():
        wait(s3.at[0:NK - 1, 0], z_send)
        wait(rw.at[0:7], w_send)

        @pl.loop(0, NK)
        def _(k):
            finish(k)

        wait(tf.at[:, 0:15], ag_send)
        wait(ov.at[:, 0], o_send)

    @pl.when(jnp.logical_not(mine))
    def _():
        wait(s3.at[0:NK - 1], z_send)
        wait(rw.at[0:8], w_send)
        wait(ov.at[:, 0], o_recv)


def local(
    right_side, lower_rows, block_inverse, ancestor_cols, pattern, ancestor_side, ancestor_inverse
):
    any_spec = pl.BlockSpec(memory_space=pl.ANY)
    vmem, dma = pltpu.VMEM, pltpu.SemaphoreType.DMA
    return pl.pallas_call(
        kernel,
        out_shape=(
            pltpu.VMEM((1, 1024, 1024), F32),
            pltpu.VMEM((1, 24, 1024), F32),
        ),
        in_specs=[pl.BlockSpec(memory_space=pltpu.SMEM)] + [any_spec] * 6,
        out_specs=(pl.BlockSpec(memory_space=vmem),) * 2,
        scratch_shapes=[
            vmem((3, 1024, 1024), B16),
            vmem((1024, 1024), B16),
            vmem((3072, 1024), B16),
            vmem((48, 768), B16),
            vmem((48, 1024), F32),
            vmem((4, NK, 1024, W), B16),
            vmem((2, 1536, W), F32),
            vmem((NK, 1536, W), B16),
            vmem((NK, 1536, W), B16),
            vmem((NK, 4, 384, W), B16),
            vmem((NK, 3, 384, W), B16),
            vmem((NK, 4, 96, W), B16),
            vmem((NK, 3, 96, W), B16),
            vmem((NK, 2, 48, W), F32),
            vmem((NK, 3, 48, W), F32),
            vmem((16, 48, W), B16),
            vmem((NK, 48, W), B16),
            vmem((NK, 16, 48, W), B16),
            vmem((NK, 2, 24, W), F32),
            dma((2,)),
            dma((8,)),
            dma((3,)),
            dma((4, NK)),
            dma, dma((NK,)),
            dma, dma((NK,)),
            dma, dma((NK - 1,)),
            dma, dma((NK - 1,)),
            dma, dma,
            dma, dma((NK,)),
            dma, dma,
        ],
        compiler_params=pltpu.CompilerParams(
            collective_id=0, has_side_effects=True, vmem_limit_bytes=52 * 1024 * 1024
        ),
        name="solve",
    )(pattern, right_side, lower_rows, block_inverse, ancestor_cols, ancestor_side, ancestor_inverse)


def solution(mesh):
    return jax.shard_map(
        local,
        mesh=mesh,
        in_specs=(
            P("leaf", "chain", None),
            P("leaf", "chain", None),
            P("leaf", "chain", None),
            P("leaf", None, "chain"),
            P("leaf", None),
            P("chain", None),
            P("chain", None),
        ),
        out_specs=(P("leaf", "chain", None), P("chain", "leaf", None)),
        check_vma=False,
    )
```

```python
import jax
import jax.numpy as jnp
from jax import lax
from jax.experimental import pallas as pl
from jax.experimental.pallas import tpu as pltpu
from jax.sharding import PartitionSpec as P

MESH = pl.DeviceIdType.MESH
ROWBLK = 128
NK = 8
W = 128
NA = 3
NW = 6
AHEAD = 5
FAR = (2, 1, 3)
B16 = jnp.bfloat16
F32 = jnp.float32


def dot(a, b):
    return jnp.dot(a, b, preferred_element_type=F32)


def wait(ref, sem):
    pltpu.make_async_copy(ref, ref, sem).wait()


def send(src, dst, ssem, rsem, leaf, chain):
    pltpu.make_async_remote_copy(
        src_ref=src,
        dst_ref=dst,
        send_sem=ssem,
        recv_sem=rsem,
        device_id=(leaf, chain),
        device_id_type=MESH,
    ).start()


def kernel(
    flags, rhs_hbm, low_hbm, inv_hbm, cols_hbm, side_hbm, ainv_hbm,
    sol, anc,
    lv, iv, cv, av, sv, blk, own, sx, rx, s1, r1, s2, r2, s3, r3, rw, st, tf, ov,
    rhs_sem, in_sem,
    blk_send, blk_recv, x_send, x_recv, s1_send, s1_recv, s2_send, s2_recv,
    z_send, z_recv, w_send, w_recv, ag_send, ag_recv, o_send, o_recv,
):
    me = lax.axis_index("leaf")
    z = lax.axis_index("chain")
    core = lax.rem(me, 2)
    chip = lax.div(me, 2)
    x = lax.div(chip, 4)
    y = lax.rem(chip, 4)
    f = x + core * (y - x)
    g = y + core * (x - y)

    def chip_of(ff, gg):
        a, b = ff * 4 + gg, gg * 4 + ff
        return a + core * (b - a)

    chip_rows = pl.ds(pl.multiple_of(chip * 48, 48), 48)

    def columns_of(k):
        return pl.ds(k * W if isinstance(k, int) else pl.multiple_of(k * W, W), W)

    def rhs_load(k):
        return pltpu.make_async_copy(
            rhs_hbm.at[0, :, columns_of(k)], sol.at[0, :, columns_of(k)], rhs_sem.at[min(k, 1)]
        )

    def low_load(j):
        return pltpu.make_async_copy(
            low_hbm.at[0, :, pl.ds(j * 1024, 1024)], lv.at[j], in_sem.at[j]
        )

    inv_load = pltpu.make_async_copy(inv_hbm.at[0], iv, in_sem.at[3])
    def cols_load(half):
        here = pl.ds(pl.multiple_of((half + (1 - 2 * half) * (1 - core)) * 1536, 1536), 1536)
        return pltpu.make_async_copy(
            cols_hbm.at[0, here, :], cv.at[half * 1536:(half + 1) * 1536], in_sem.at[4 + half]
        )

    side_load = pltpu.make_async_copy(side_hbm.at[chip_rows, :], sv, in_sem.at[6])
    ainv_load = pltpu.make_async_copy(ainv_hbm.at[chip_rows, :], av, in_sem.at[7])
    inv_load.start()
    rhs_load(0).start()

    barrier = pltpu.get_barrier_semaphore()

    def greet(leaf, chain):
        pl.semaphore_signal(barrier, inc=1, device_id=(leaf, chain), device_id_type=MESH)

    partner = me + 1 - 2 * core
    greet(partner, z)
    for d in range(1, 4):
        greet(me, lax.rem(z + d, 4))
        greet(chip_of(lax.rem(f + d, 4), g) * 2 + core, z)
        greet(chip_of(f, lax.rem(g + d, 4)) * 2 + core, z)

    def solve(k):
        solved = dot(iv[...], sol[0, :, columns_of(k)].astype(B16))
        blk[z, k] = solved.astype(B16)
        sol[0, :, columns_of(k)] = solved

    def send_block(j, k, slot, to):
        send(blk.at[j, k], blk.at[j, k], blk_send.at[slot], blk_recv.at[j, k], me, to)

    def send_solved(k):
        @pl.when(z < 3)
        def _():
            send_block(z, k, 0, z + 1)

        @pl.when(jnp.logical_or(z == 0, jnp.logical_and(z == 1, k >= NA)))
        def _():
            send_block(z, k, 1, lax.rem(z + 3, 4))

    def pass_block0(k):
        wait(blk.at[0, k], blk_recv.at[0, k])
        send_block(0, k, 2, 2)
        sol[0, :, columns_of(k)] -= dot(lv[0], blk[0, k])

    inv_load.wait()
    rhs_load(0).wait()
    for k in range(1, NK):
        rhs_load(k).start()
    for j in range(3):
        @pl.when(z > j)
        def _():
            low_load(j).start()
    cols_load(0).start()
    cols_load(1).start()
    side_load.start()
    ainv_load.start()

    @pl.when(z == 0)
    def _():
        solve(0)

    pl.semaphore_wait(barrier, 10)

    @pl.when(z == 0)
    def _():
        send_solved(0)

    wait(sol.at[0, :, W:NK * W], rhs_sem.at[1])

    for j in range(3):
        @pl.when(z > j)
        def _():
            low_load(j).wait()

    @pl.when(z == 3)
    def _():
        @pl.loop(0, AHEAD)
        def _(k):
            pass_block0(k)

    def chain(k):
        @pl.loop(lax.div(z, 3), z)
        def _(j):
            wait(blk.at[j, k], blk_recv.at[j, k])

            @pl.when(jnp.logical_and(jnp.logical_and(z == 2, j == 1), k < NA))
            def _():
                send_block(1, k, 2, 3)

            sol[0, :, columns_of(k)] -= dot(lv[j], blk[j, k])

        @pl.when(z + k > 0)
        def _():
            solve(k)
            send_solved(k)

    def mask_columns():
        for half in range(2):
            cols_load(half).wait()

        @pl.loop(0, 24)
        def _(i):
            rows = pl.ds(pl.multiple_of(i * ROWBLK, ROWBLK), ROWBLK)
            entry = lax.rem(i + 12 * (1 - core), 24)
            cv[rows, :] = cv[rows, :] * flags[0, entry].astype(F32).astype(B16)

    def product(chunks):
        solved = jnp.concatenate([blk[z, k] for k in chunks], axis=1)
        part = dot(cv[0:1536, :], solved)
        for i, k in enumerate(chunks):
            sx[k] = part[:, i * W:(i + 1) * W].astype(B16)
        part = dot(cv[1536:3072, :], solved)
        for i in range(len(chunks)):
            own[i] = part[:, i * W:(i + 1) * W]
        for k in chunks:
            send(sx.at[k], rx.at[k], x_send, x_recv.at[k], partner, z)

    def pair_sum(k, slot):
        wait(rx.at[k], x_recv.at[k])
        for ff in range(4):
            for ci in range(2):
                for gg in range(4):
                    rows = pl.ds(pl.multiple_of(ci * 768 + chip_of(ff, gg) * 48, 48), 48)
                    total = own[slot, rows, :] + rx[k, rows, :].astype(F32)
                    at = ci * 192 + gg * 48
                    s1[k, ff, at:at + 48, :] = total.astype(B16)
        for d in FAR:
            to = lax.rem(f + d, 4)
            send(
                s1.at[k, to], r1.at[k, d - 1], s1_send, s1_recv.at[k],
                chip_of(to, g) * 2 + core, z,
            )

    def first_total(k):
        wait(r1.at[k], s1_recv.at[k])
        for ci in range(2):
            for gg in range(4):
                at = ci * 192 + gg * 48
                total = s1[k, f, at:at + 48, :].astype(F32)
                for d in range(3):
                    total += r1[k, d, at:at + 48, :].astype(F32)
                s2[k, gg, ci * 48:(ci + 1) * 48, :] = total.astype(B16)

    def first_sum(k):
        first_total(k)
        for d in FAR:
            to = lax.rem(g + d, 4)
            send(
                s2.at[k, to], r2.at[k, d - 1], s2_send, s2_recv.at[k],
                chip_of(f, to) * 2 + core, z,
            )

    def wide_send(k):
        first_total(k)
        slot = z * 4 + g
        for d in FAR + (0,):
            for ci in range(2):
                owner = core * 2 + ci
                to = lax.rem(g + d, 4)
                piece = s2.at[k, to, ci * 48:(ci + 1) * 48, :]

                def go():
                    send(
                        piece, rw.at[k - NW, slot], w_send, w_recv.at[k - NW],
                        chip_of(f, to) * 2 + core, owner,
                    )

                if d > 0:
                    go()
                else:
                    pl.when(owner != z)(go)

                    @pl.when(owner == z)
                    def _():
                        rw[k - NW, slot] = piece[...]

    def second_sum(k):
        wait(r2.at[k], s2_recv.at[k])
        for ci in range(2):
            at = ci * 48
            total = s2[k, g, at:at + 48, :].astype(F32)
            for d in range(3):
                total += r2[k, d, at:at + 48, :].astype(F32)
            s3[k, ci] = total
            owner = core * 2 + ci
            away = lax.rem(owner - z + 4, 4)

            @pl.when(away != 0)
            def _():
                send(
                    s3.at[k, ci], r3.at[k, away - 1], z_send, z_recv.at[k],
                    me, owner,
                )

    mine = lax.div(z, 2) == core

    def wide_sum(k):
        wait(rw.at[k - NW, 0:15], w_recv.at[k - NW])
        total = rw[k - NW, 0].astype(F32)
        for i in range(1, 16):
            total += rw[k - NW, i].astype(F32)
        gather(k, total)

    def last_sum(k):
        wait(r3.at[k], z_recv.at[k])
        total = s3[k, z - 2 * core]
        for d in range(3):
            total += r3[k, d]
        gather(k, total)

    def gather(k, total):
        here = sv[:, pl.ds(pl.multiple_of(k * W, W), W)]
        st[k] = (here - total).astype(B16)

        for d in FAR + (0,):
            for e in FAR + (0,):
                if d + e > 0:
                    to = chip_of(lax.rem(f + d, 4), lax.rem(g + e, 4)) * 2 + core
                    send(st.at[k], tf.at[k, chip], ag_send, ag_recv.at[k], to, z)

        tf[k, chip] = st[k]

    def finish(k):
        wait(tf.at[k, 0:15], ag_recv.at[k])
        result = dot(av[...], jnp.concatenate([tf[k, i] for i in range(16)], axis=0))
        ov[k, 0] = result[:24]
        ov[k, 1] = result[24:]
        send(
            ov.at[k, 1 - core], anc.at[0, :, columns_of(k)], o_send, o_recv,
            partner, z,
        )
        anc[0, :, columns_of(k)] = ov[k, core]

    def last_plane(step, chunks):
        @pl.when(jnp.logical_and(mine, z == 3))
        def _():
            for k in chunks:
                step(k)

    @pl.loop(0, 3)
    def _(m):
        for i in range(2):
            k = m * 2 + i

            chain(k)

            @pl.when(jnp.logical_and(z == 3, k + AHEAD < NK))
            def _():
                pass_block0(k + AHEAD)

        @pl.when(m == 0)
        def _():
            mask_columns()
            side_load.wait()
            ainv_load.wait()

        product((m * 2, m * 2 + 1))

        @pl.when(m >= 1)
        def _():
            for i in range(2):
                first_sum(m * 2 - 2 + i)

        for i in range(2):
            pair_sum(m * 2 + i, i)

        @pl.when(m >= 2)
        def _():
            for i in range(2):
                second_sum(m * 2 - 4 + i)
            last_plane(last_sum, (0,))

    chain(6)
    product((6,))
    second_sum(2)
    second_sum(3)
    chain(7)
    pair_sum(6, 0)
    product((7,))
    first_sum(4)
    first_sum(5)
    pair_sum(7, 0)

    @pl.when(z == 0)
    def _():
        @pl.loop(NA, NK)
        def _(k):
            wait(blk.at[1, k], blk_recv.at[1, k])
            send_block(1, k, 2, 3)

    wide_send(6)
    second_sum(4)
    second_sum(5)
    wide_send(7)

    @pl.when(jnp.logical_and(mine, z != 3))
    def _():
        @pl.loop(0, NW)
        def _(k):
            last_sum(k)

    @pl.when(mine)
    def _():
        wide_sum(6)
        wide_sum(7)

    last_plane(last_sum, range(1, NW))

    @pl.when(z < 3)
    def _():
        wait(blk.at[0], blk_send.at[0])

    @pl.when(z == 0)
    def _():
        wait(blk.at[0], blk_send.at[1])
        wait(blk.at[0, NA:NK], blk_send.at[2])

    @pl.when(z == 1)
    def _():
        wait(blk.at[0, NA:NK], blk_send.at[1])

    @pl.when(z == 2)
    def _():
        wait(blk.at[0, 0:NA], blk_send.at[2])

    @pl.when(z == 3)
    def _():
        wait(blk.at[0], blk_send.at[2])

    wait(sx, x_send)
    wait(r1, s1_send)
    wait(r2.at[0:NW], s2_send)

    @pl.when(mine)
    def _():
        wait(s3.at[0:NW, 0], z_send)
        wait(rw.at[:, 0:7], w_send)

        @pl.loop(0, NK)
        def _(k):
            finish(k)

        wait(tf.at[:, 0:15], ag_send)
        wait(ov.at[:, 0], o_send)

    @pl.when(jnp.logical_not(mine))
    def _():
        wait(s3.at[0:NW], z_send)
        wait(rw.at[:, 0:8], w_send)
        wait(ov.at[:, 0], o_recv)


def local(
    right_side, lower_rows, block_inverse, ancestor_cols, pattern, ancestor_side, ancestor_inverse
):
    any_spec = pl.BlockSpec(memory_space=pl.ANY)
    vmem, dma = pltpu.VMEM, pltpu.SemaphoreType.DMA
    return pl.pallas_call(
        kernel,
        out_shape=(
            pltpu.VMEM((1, 1024, 1024), F32),
            pltpu.VMEM((1, 24, 1024), F32),
        ),
        in_specs=[pl.BlockSpec(memory_space=pltpu.SMEM)] + [any_spec] * 6,
        out_specs=(pl.BlockSpec(memory_space=vmem),) * 2,
        scratch_shapes=[
            vmem((3, 1024, 1024), B16),
            vmem((1024, 1024), B16),
            vmem((3072, 1024), B16),
            vmem((48, 768), B16),
            vmem((48, 1024), F32),
            vmem((4, NK, 1024, W), B16),
            vmem((2, 1536, W), F32),
            vmem((NK, 1536, W), B16),
            vmem((NK, 1536, W), B16),
            vmem((NK, 4, 384, W), B16),
            vmem((NK, 3, 384, W), B16),
            vmem((NK, 4, 96, W), B16),
            vmem((NK, 3, 96, W), B16),
            vmem((NK, 2, 48, W), F32),
            vmem((NK, 3, 48, W), F32),
            vmem((NK - NW, 16, 48, W), B16),
            vmem((NK, 48, W), B16),
            vmem((NK, 16, 48, W), B16),
            vmem((NK, 2, 24, W), F32),
            dma((2,)),
            dma((8,)),
            dma((3,)),
            dma((4, NK)),
            dma, dma((NK,)),
            dma, dma((NK,)),
            dma, dma((NW,)),
            dma, dma((NW,)),
            dma, dma((NK - NW,)),
            dma, dma((NK,)),
            dma, dma,
        ],
        compiler_params=pltpu.CompilerParams(
            collective_id=0, has_side_effects=True, vmem_limit_bytes=52 * 1024 * 1024
        ),
        name="solve",
    )(pattern, right_side, lower_rows, block_inverse, ancestor_cols, ancestor_side, ancestor_inverse)


def solution(mesh):
    return jax.shard_map(
        local,
        mesh=mesh,
        in_specs=(
            P("leaf", "chain", None),
            P("leaf", "chain", None),
            P("leaf", "chain", None),
            P("leaf", None, "chain"),
            P("leaf", None),
            P("chain", None),
            P("chain", None),
        ),
        out_specs=(P("leaf", "chain", None), P("chain", "leaf", None)),
        check_vma=False,
    )
```
